256 devices in a mesh: term: 8 (over x, z_lo), sector: 32 (over z_hi, y, core).
Axes of the slice: x: 4, y: 4, z: 8 (z_hi: 4, z_lo: 2; z = z_hi * 2 + z_lo), core: 2. Of those that a mesh axis runs over, the one named last changes fastest.
Arguments:
- psi_start: bfloat16 [256, 256, 256], P('sector'), may hold values from -6 to 6
- left_env: bfloat16 [24, 256, 256, 256], P('term', 'sector')
- right_env: bfloat16 [24, 256, 256, 256], P('term', 'sector')
- connect: int32 [24, 256], P('term', 'sector'), may hold values from 0 to 255, as said below
- sector_dims: int32 [2, 256], P(None, 'sector'), may hold values from 64 to 256
- precond: bfloat16 [256, 256, 256], P('sector'), may hold values from 0.5 to 4
Outputs:
- projected: float32 [3, 3], replicated
- last_vector: float32 [256, 256, 256], P('sector', 'term')
- new_env: bfloat16 [24, 256, 256, 256], P('term', 'sector')
The draws below stay inside these ranges and needn't reach their ends.
Inputs may be any that keep to these rules, and one draw needn't show every extreme that they name: connect[t, s] differs from s by at most 8.
All inputs are finite; a program needn't handle non-finite values.
Results may differ from the reference program's by a relative error of at most 0.012.
Values may be sent and summed in bfloat16 or wider, within the bound.
No kernel may reach another device: no remote copies, remote signals or barrier semaphores. Data moves between devices by JAX's collectives and lax.ppermute only.
A program may use at most 128 MiB of HBM per device.

```python
import math
import jax
import jax.numpy as jnp
from jax import lax

DB = 256
SD = 8
TD = 3
SECTORS = 256
TERMS = 24


identity_weight = 0.06


drawn_spread = 0.5


shifted_spread = 0.3


def shift_terms():
    return jnp.arange(TERMS) % TD == TD - 1


def unit_diagonal():
    row_ids = lax.broadcasted_iota(jnp.int32, (DB, DB), 0)
    col_ids = lax.broadcasted_iota(jnp.int32, (DB, DB), 1)
    return (row_ids == col_ids).astype(jnp.float32)


def draw_left_env(key, part):
    noise_key, device_key, sector_key = jax.random.split(jax.random.fold_in(key, 17), 3)
    full_shape = (TERMS, SECTORS, DB, DB)
    noise = jax.random.normal(noise_key, full_shape, jnp.float32)
    scaled = noise * DB ** (-0.5)
    device_scale = jnp.exp(jax.random.uniform(device_key, (SECTORS // SD,), jnp.float32, math.log(0.1), math.log(1.0)))
    sector_scale = jnp.exp(jax.random.uniform(sector_key, (SECTORS,), jnp.float32, math.log(0.6), math.log(1.6)))
    energies = jnp.repeat(device_scale, SD) * sector_scale
    shifted = identity_weight * (energies[None, :, None, None] * unit_diagonal()[None, None] + shifted_spread * scaled)
    drawn = drawn_spread * scaled
    return jnp.where(shift_terms()[:, None, None, None], shifted, drawn).astype(jnp.bfloat16)


def draw_right_env(key, part):
    noise_key = jax.random.fold_in(key, 29)
    full_shape = (TERMS, SECTORS, DB, DB)
    noise = jax.random.normal(noise_key, full_shape, jnp.float32)
    scaled = noise * DB ** (-0.5)
    shift_count = TERMS // TD
    right_scale = 2.0 / (shift_count * identity_weight)
    shifted = right_scale * (unit_diagonal()[None, None] + shifted_spread * scaled)
    drawn = drawn_spread * scaled
    return jnp.where(shift_terms()[:, None, None, None], shifted, drawn).astype(jnp.bfloat16)


def draw_connect(key, part):
    offsets = jax.random.randint(jax.random.fold_in(key, 5), (TERMS, SECTORS), -SD, SD + 1)
    places = jnp.arange(SECTORS)[None, :]
    term_ids = jnp.arange(TERMS)[:, None]
    lower = (places % SD == 0) & (term_ids == 0)
    upper = (places % SD == SD - 1) & (term_ids == 1)
    offsets = jnp.where(lower, -SD, jnp.where(upper, SD, offsets))
    offsets = jnp.where(term_ids % TD == TD - 1, 0, offsets)
    return jnp.clip(places + offsets, 0, SECTORS - 1).astype(jnp.int32)


def plant(array, key, low, top_value):
    longest = array.shape.index(max(array.shape))
    spots = []
    for shift in (0, 1):
        where = [jax.random.randint(jax.random.fold_in(key, axis), (), 0, length) for axis, length in enumerate(array.shape)]
        where[longest] = (where[longest] + shift) % array.shape[longest]
        spots.append(tuple(where))
    return array.at[spots[0]].set(low).at[spots[1]].set(top_value)


def steps_of(key, dims, cuts, low, top_value):
    def one(dim, blocks):
        heights = jax.random.uniform(jax.random.fold_in(jax.random.fold_in(key, 6), dim), (blocks,), jnp.float32, low / len(cuts), top_value / len(cuts))
        return jnp.repeat(jnp.exp(heights), dims[dim] // blocks).reshape((-1,) + (1,) * (len(dims) - dim - 1))

    factor_of = one(*cuts[0])
    for cut in cuts[1:]:
        factor_of = factor_of * one(*cut)
    return factor_of


def gaussian(own_key, dims, spread, reach, cuts=(), dtype=jnp.bfloat16):
    factor_of = steps_of(own_key, dims, cuts, -0.22, 0.18) if cuts else 1.0
    array = jax.random.normal(own_key, dims, jnp.float32) * spread * factor_of
    return jnp.minimum(jnp.maximum(array, -reach), reach).astype(dtype)


def setup_inputs(seed: int = 0) -> dict:
    arg_keys = jax.random.split(jax.random.key(seed), 7)
    psi_start = gaussian(arg_keys[0], (SECTORS, DB, DB), 1.0, 6.0, ((0, 32),))
    left_env = draw_left_env(jax.random.fold_in(arg_keys[6], 71), 0)
    right_env = draw_right_env(jax.random.fold_in(arg_keys[6], 71), 0)
    connect = draw_connect(jax.random.fold_in(arg_keys[6], 71), 0)
    sector_dims = plant(jax.random.randint(arg_keys[4], (2, SECTORS), DB // 4, DB + 1), jax.random.fold_in(arg_keys[4], 1), DB // 4, DB).astype(jnp.int32)
    precond = jnp.clip(jnp.exp(math.log(4.0) - 2.0794415 * jax.random.uniform(arg_keys[5], (SECTORS, DB, DB), jnp.float32) ** steps_of(arg_keys[5], (SECTORS, DB, DB), ((0, 32),), -0.2, 0.2)), 0.5, 4.0).astype(jnp.bfloat16)
    return dict(psi_start=psi_start, left_env=left_env, right_env=right_env, connect=connect, sector_dims=sector_dims, precond=precond)


epsilon = 1e-06

def block_mask(sector_dims):
    row_ids = lax.broadcasted_iota(jnp.int32, (SECTORS, DB, DB), 1)
    col_ids = lax.broadcasted_iota(jnp.int32, (SECTORS, DB, DB), 2)
    keep = (row_ids < sector_dims[0][:, None, None]) & (col_ids < sector_dims[1][:, None, None])
    return keep.astype(jnp.float32)

def apply_terms(vector_b, left_env, right_env, connect, with_env):

    def one_term(total, pieces):
        left_one, right_one, source_one = pieces
        source = vector_b[source_one]
        half = jnp.einsum('sij,sjk->sik', left_one.astype(jnp.float32), source.astype(jnp.float32)).astype(jnp.bfloat16)
        total = total + jnp.einsum('sik,slk->sil', half.astype(jnp.float32), right_one.astype(jnp.float32))
        if with_env:
            env_one = jnp.einsum('sji,sjk->sik', vector_b.astype(jnp.float32), half.astype(jnp.float32)) * DB ** (-0.5)
            return (total, env_one.astype(jnp.bfloat16))
        return (total, None)
    return lax.scan(one_term, jnp.zeros((SECTORS, DB, DB), jnp.float32), (left_env, right_env, connect))

def reference(psi_start, left_env, right_env, connect, sector_dims, precond):
    mask = block_mask(sector_dims)
    entries = float(SECTORS * DB * DB)

    def inner(first, second):
        return jnp.sum(first * second) / entries
    vector = mask * psi_start.astype(jnp.float32)
    vector = vector / jnp.sqrt(inner(vector, vector) + epsilon)
    basis = [vector]
    sigmas = []
    new_env = None
    for which in range(3):
        vector_b = basis[which].astype(jnp.bfloat16)
        if which < 2:
            total, unused = apply_terms(vector_b, left_env, right_env, connect, False)
        else:
            total, new_env = apply_terms(vector_b, left_env, right_env, connect, True)
        sigma = total * mask
        sigmas.append(sigma)
        if which < 2:
            theta = inner(basis[which], sigma)
            corr = (sigma - theta * basis[which]) / precond.astype(jnp.float32)
            correlations = [inner(member, corr) for member in basis]
            for member, weight in zip(basis, correlations):
                corr = corr - weight * member
            corr = corr / jnp.sqrt(inner(corr, corr) + epsilon)
            basis.append(corr)
    projected = jnp.stack([jnp.stack([inner(basis[row], sigmas[col]) for col in range(3)]) for row in range(3)])
    return (projected, basis[2], new_env)
```

```python
import jax
import jax.numpy as jnp
from jax import lax
from jax.experimental import pallas as pl
from jax.experimental.pallas import tpu as pltpu
from jax.sharding import PartitionSpec as P

epsilon = 1e-06
f32 = jnp.float32
bf16 = jnp.bfloat16


def to_everyone(x, axis):
    devices = lax.axis_size(axis)
    return lax.all_to_all(jnp.broadcast_to(x[None], (devices, *x.shape)), axis, 0, 0, tiled=True)


def neighbours(block):
    count = lax.axis_size("sector")
    forward = [(i, i + 1) for i in range(count - 1)]
    backward = [(i + 1, i) for i in range(count - 1)]
    return lax.ppermute(block, "sector", forward), lax.ppermute(block, "sector", backward)


def row_of(total_ref, entries):
    return jnp.sum(total_ref[...], axis=0, keepdims=True) * (1.0 / entries)


def one(row, k):
    return row[:, k : k + 1]


def first_scale(row0):
    return 1.0 / jnp.sqrt(one(row0, 0) + epsilon)


def second_weights(row0, row1):
    inv = first_scale(row0)
    theta = inv * one(row1, 0)
    a = inv * one(row1, 1)
    b = inv * inv * one(row1, 2)
    aa = one(row1, 3)
    ab = inv * one(row1, 4)
    bb = inv * inv * one(row1, 5)
    vv = inv * inv * one(row0, 0)
    o = a - theta * b
    length = aa + theta * theta * bb + o * o * vv - 2.0 * theta * ab - 2.0 * o * a + 2.0 * theta * o * b
    r = 1.0 / jnp.sqrt(jnp.maximum(length, 0.0) + epsilon)
    return r, -r * theta * inv, -r * o * inv


def third_weights(row0, row2):
    inv = first_scale(row0)
    theta = one(row2, 0)
    v1a = inv * one(row2, 1)
    v1b = inv * one(row2, 2)
    v2a = one(row2, 3)
    v2b = one(row2, 4)
    aa = one(row2, 5)
    ab = one(row2, 6)
    bb = one(row2, 7)
    v1v2 = inv * one(row2, 8)
    v2v2 = one(row2, 9)
    v1v1 = inv * inv * one(row0, 0)
    o1 = v1a - theta * v1b
    o2 = v2a - theta * v2b
    length = (
        aa
        - 2.0 * theta * ab
        + theta * theta * bb
        - 2.0 * o1 * o1
        - 2.0 * o2 * o2
        + o1 * o1 * v1v1
        + 2.0 * o1 * o2 * v1v2
        + o2 * o2 * v2v2
    )
    r = 1.0 / jnp.sqrt(jnp.maximum(length, 0.0) + epsilon)
    return r, -r * theta, -r * o1 * inv, -r * o2


def whole(ref, s):
    block = ref[:, s]
    return block.reshape(block.shape[0] * block.shape[1], block.shape[2]).astype(f32)


def fold(x):
    return jnp.sum(x.reshape(x.shape[0] // 8, 8, x.shape[1]), axis=0)


def row_from(sums):
    lane = lax.broadcasted_iota(jnp.int32, (1, 128), 1)
    row = jnp.zeros((1, 128), f32)
    for k, total in enumerate(sums):
        row = row + jnp.where(lane == k, jnp.sum(total), 0.0)
    return row


def keep_of(dims_ref, s, width):
    rows = lax.broadcasted_iota(jnp.int32, (width, width), 0)
    cols = lax.broadcasted_iota(jnp.int32, (width, width), 1)
    return (rows < dims_ref[0, s]) & (cols < dims_ref[1, s])


def start_kernel(dims_ref, psi_ref, out_ref, row_ref):
    blocks, width = psi_ref.shape[0], psi_ref.shape[1]

    def body(s, acc):
        x = jnp.where(keep_of(dims_ref, s, width), psi_ref[s].astype(f32), 0.0)
        out_ref[s] = x.astype(bf16)
        return acc + fold(x * x)

    acc = lax.fori_loop(0, blocks, body, jnp.zeros((8, width), f32))
    row_ref[...] = row_from([acc])


def gram1_kernel(sig_ref, psi_ref, d_ref, row_ref):
    blocks, width = psi_ref.shape[0], psi_ref.shape[1]

    def body(s, acc):
        sig = whole(sig_ref, s)
        psi = psi_ref[s].astype(f32)
        rd = 1.0 / d_ref[s].astype(f32)
        a, b = sig * rd, psi * rd
        terms = (psi * sig, psi * a, psi * b, a * a, a * b, b * b)
        return tuple(t + fold(x) for t, x in zip(acc, terms))

    acc = lax.fori_loop(0, blocks, body, (jnp.zeros((8, width), f32),) * 6)
    row_ref[...] = row_from(acc)


def gram2_kernel(entries, tot0, tot1, sig2_ref, sig1_ref, psi_ref, d_ref, row_ref):
    blocks, width = psi_ref.shape[0], psi_ref.shape[1]
    p, q, w = second_weights(row_of(tot0, entries), row_of(tot1, entries))

    def body(s, acc):
        sig2, sig1 = whole(sig2_ref, s), whole(sig1_ref, s)
        psi = psi_ref[s].astype(f32)
        rd = 1.0 / d_ref[s].astype(f32)
        v2 = (p * sig1 + q * psi) * rd + w * psi
        a, b = sig2 * rd, v2 * rd
        terms = (
            v2 * sig2,
            psi * a,
            psi * b,
            v2 * a,
            v2 * b,
            a * a,
            a * b,
            b * b,
            psi * v2,
            v2 * v2,
            psi * sig2,
            v2 * sig1,
        )
        return tuple(t + fold(x) for t, x in zip(acc, terms))

    acc = lax.fori_loop(0, blocks, body, (jnp.zeros((8, width), f32),) * 12)
    row_ref[...] = row_from(acc)


def dot(a, b, ca, cb):
    return lax.dot_general(a, b, (((ca,), (cb,)), ((), ())), preferred_element_type=f32)


def product_kernel(stage, entries, *refs):
    conn_ref, dims_ref = refs[:2]
    refs = refs[2:]
    tots, refs = refs[:stage], refs[stage:]
    psi, refs = refs[:3], refs[3:]
    d = sig1 = sig2 = (None, None, None)
    if stage > 1:
        d, sig1, refs = refs[:3], refs[3:6], refs[6:]
    if stage > 2:
        sig2, refs = refs[:3], refs[3:]
    left_ref, right_ref = refs[:2]
    if stage < 3:
        out_ref, vb_ref = refs[2:]
    else:
        env_ref, last_ref, row_ref, vb_ref, acc_ref = refs[2:]
    step = pl.program_id(0)
    blocks, width = psi[0].shape[0], psi[0].shape[1]
    rows = [row_of(t, entries) for t in tots]

    def vectors(seg, s):
        x = psi[seg][s].astype(f32)
        inv = first_scale(rows[0])
        if stage == 1:
            return [x * inv], [], x
        p, q, w = second_weights(rows[0], rows[1])
        rd = 1.0 / d[seg][s].astype(f32)
        s1 = whole(sig1[seg], s)
        v2 = (p * s1 + q * x) * rd + w * x
        if stage == 2:
            return [x * inv, v2], [s1], x
        p, q, w, y = third_weights(rows[0], rows[2])
        s2 = whole(sig2[seg], s)
        v3 = (p * s2 + q * v2) * rd + w * x + y * v2
        return [x * inv, v2, v3], [s1, s2], x

    @pl.when(step == 0)
    def _():
        for seg in range(3):

            def body(s, carry, seg=seg):
                vb_ref[seg * blocks + s] = vectors(seg, s)[0][-1].astype(bf16)
                return carry

            lax.fori_loop(0, blocks, body, 0)
        if stage == 3:
            acc_ref[...] = jnp.zeros_like(acc_ref)

    total = jnp.zeros((width, width), f32)
    if stage == 3:
        own = vb_ref[blocks + step]
        own_t = own.T
    for t in range(left_ref.shape[0]):
        half = dot(left_ref[t, 0], vb_ref[conn_ref[t, step]], 1, 0).astype(bf16)
        total = total + dot(half, right_ref[t, 0], 1, 1)
        if stage == 3:
            env_ref[t, 0] = (dot(own_t, half, 1, 0) * width ** (-0.5)).astype(bf16)
    if stage < 3:
        total = jnp.where(keep_of(dims_ref, step, width), total, 0.0).astype(bf16)
        out_ref[:, 0] = total.reshape(out_ref.shape[0], out_ref.shape[2], width)
    else:
        vs, sigs, _ = vectors(1, step)
        pieces = sig1[1].shape[0]
        share = width // pieces
        last_ref[0] = vs[2].reshape(pieces, share, width)
        terms = (vs[0] * total, vs[1] * total, vs[2] * total, vs[2] * sigs[0], vs[2] * sigs[1])
        for k, x in enumerate(terms):
            acc_ref[k] += fold(x)

        @pl.when(step == blocks - 1)
        def _():
            row_ref[...] = row_from([acc_ref[k] for k in range(5)])


def product(stage, entries, pieces, conn, dims, tots, vectors, left, right):
    terms, blocks, width = left.shape[:3]
    share = width // pieces
    smem = pl.BlockSpec(memory_space=pltpu.SMEM)
    vmem = pl.BlockSpec(memory_space=pltpu.VMEM)
    env_spec = pl.BlockSpec((terms, 1, width, width), lambda s: (0, s, 0, 0))
    scratch = [pltpu.VMEM((3 * blocks, width, width), bf16)]
    if stage < 3:
        out_shape = jax.ShapeDtypeStruct((pieces, blocks, share, width), bf16)
        out_specs = pl.BlockSpec((pieces, 1, share, width), lambda s: (0, s, 0, 0))
    else:
        out_shape = (
            jax.ShapeDtypeStruct(left.shape, bf16),
            jax.ShapeDtypeStruct((blocks, pieces, share, width), f32),
            jax.ShapeDtypeStruct((1, 128), f32),
        )
        out_specs = (
            env_spec,
            pl.BlockSpec((1, pieces, share, width), lambda s: (s, 0, 0, 0)),
            pl.BlockSpec((1, 128), lambda s: (0, 0)),
        )
        scratch.append(pltpu.VMEM((5, 8, width), f32))
    return pl.pallas_call(
        lambda *refs: product_kernel(stage, entries, *refs),
        grid=(blocks,),
        in_specs=[smem, smem] + [vmem] * (len(tots) + len(vectors)) + [env_spec, env_spec],
        out_specs=out_specs,
        out_shape=out_shape,
        scratch_shapes=scratch,
        name=f"product_{stage}",
        compiler_params=pltpu.CompilerParams(vmem_limit_bytes=48 << 20),
    )(conn, dims, *tots, *vectors, left, right)


def call_small(kernel, dims, arrays, out_shape, name):
    smem = pl.BlockSpec(memory_space=pltpu.SMEM)
    vmem = pl.BlockSpec(memory_space=pltpu.VMEM)
    return pl.pallas_call(
        kernel,
        in_specs=[smem] * len(dims) + [vmem] * len(arrays),
        out_specs=jax.tree.map(lambda _: vmem, out_shape),
        out_shape=out_shape,
        name=name,
        compiler_params=pltpu.CompilerParams(vmem_limit_bytes=32 << 20),
    )(*dims, *arrays)


def on_device(psi_start, left_env, right_env, connect, sector_dims, precond):
    blocks, width = psi_start.shape[:2]
    devices = lax.axis_size("sector")
    pieces = lax.axis_size("term")
    share = width // pieces
    entries = float(blocks * devices * width * width)
    conn = connect - (lax.axis_index("sector") * blocks - blocks)
    row = jax.ShapeDtypeStruct((1, 128), f32)

    def totals(values):
        return to_everyone(values[0], "sector")

    def gathered(partial):
        arrived = lax.all_to_all(partial, "term", 0, 0, tiled=True)
        mine = arrived.astype(f32).sum(axis=0).astype(bf16)
        return to_everyone(mine, "term")

    psi, row0 = call_small(
        start_kernel, [sector_dims], [psi_start], (jax.ShapeDtypeStruct(psi_start.shape, bf16), row), "start"
    )
    psi_low, psi_high = neighbours(psi)
    tot0 = totals(row0)
    d_low, d_high = neighbours(precond)
    psis = (psi_low, psi, psi_high)
    ds = (d_low, precond, d_high)
    args = (left_env, right_env)

    part1 = product(1, entries, pieces, conn, sector_dims, (tot0,), psis, *args)
    sig1 = gathered(part1)
    low, high = neighbours(sig1)
    row1 = call_small(gram1_kernel, [], [sig1, psi, precond], row, "gram_1")
    tot1 = totals(row1)
    sig1s = (low, sig1, high)

    part2 = product(2, entries, pieces, conn, sector_dims, (tot0, tot1), (*psis, *ds, *sig1s), *args)
    sig2 = gathered(part2)
    low, high = neighbours(sig2)
    row2 = call_small(
        lambda *refs: gram2_kernel(entries, *refs), [], [tot0, tot1, sig2, sig1, psi, precond], row, "gram_2"
    )
    tot2 = totals(row2)
    sig2s = (low, sig2, high)

    env, last, row3 = product(
        3, entries, pieces, conn, sector_dims, (tot0, tot1, tot2), (*psis, *ds, *sig1s, *sig2s), *args
    )
    lane = lax.broadcasted_iota(jnp.int32, (1, 128), 1)
    row3 = jnp.where(lane < 3, row3, row3 / pieces)
    by_term = to_everyone(row3[0], "term").sum(axis=0)
    last_row = to_everyone(by_term, "sector").sum(axis=0) / entries
    inv = 1.0 / jnp.sqrt(tot0[:, 0].sum() / entries + epsilon)
    r1 = tot1.sum(axis=0) / entries
    r2 = tot2.sum(axis=0) / entries
    projected = jnp.stack(
        [inv * r1[0], inv * r2[10], last_row[0], r2[11], r2[0], last_row[1], last_row[3], last_row[4], last_row[2]]
    ).reshape(3, 3)
    mine = lax.dynamic_slice_in_dim(last, lax.axis_index("term"), 1, 1)
    last_vector = mine.reshape(blocks, share, width)
    return (projected, last_vector, env)


def solution(mesh):
    placed = (
        P("sector", None, None),
        P("term", "sector", None, None),
        P("term", "sector", None, None),
        P("term", "sector"),
        P(None, "sector"),
        P("sector", None, None),
    )
    return jax.shard_map(
        on_device,
        mesh=mesh,
        in_specs=placed,
        out_specs=(P(), P("sector", "term", None), P("term", "sector", None, None)),
        check_vma=False,
    )
```

```python
import jax
import jax.numpy as jnp
from jax import lax
from jax.experimental import pallas as pl
from jax.experimental.pallas import tpu as pltpu
from jax.sharding import PartitionSpec as P

epsilon = 1e-06
f32 = jnp.float32
bf16 = jnp.bfloat16


def to_everyone(x, axis):
    devices = lax.axis_size(axis)
    return lax.all_to_all(jnp.broadcast_to(x[None], (devices, *x.shape)), axis, 0, 0, tiled=True)


def swapped(block, first):
    pairs = [(i, i + 1) for i in range(first, lax.axis_size("sector") - 1, 2)]
    return lax.ppermute(block, "sector", pairs + [(j, i) for i, j in pairs])


def row_of(total_ref, entries):
    return jnp.sum(total_ref[...], axis=0, keepdims=True) * (1.0 / entries)


def one(row, k):
    return row[:, k : k + 1]


def first_scale(row1):
    return 1.0 / jnp.sqrt(one(row1, 6) + epsilon)


def second_weights(row1):
    inv = first_scale(row1)
    theta, a, b, aa, ab, bb, vv = (inv * inv * one(row1, k) for k in range(7))
    o = a - theta * b
    length = aa + theta * theta * bb + o * o * vv - 2.0 * theta * ab - 2.0 * o * a + 2.0 * theta * o * b
    r = 1.0 / jnp.sqrt(jnp.maximum(length, 0.0) + epsilon)
    return r * inv, -r * theta * inv, -r * o * inv


def third_weights(row1, row2):
    inv = first_scale(row1)
    theta = one(row2, 0)
    v1a = inv * one(row2, 1)
    v1b = inv * one(row2, 2)
    v2a = one(row2, 3)
    v2b = one(row2, 4)
    aa = one(row2, 5)
    ab = one(row2, 6)
    bb = one(row2, 7)
    v1v2 = inv * one(row2, 8)
    v2v2 = one(row2, 9)
    v1v1 = inv * inv * one(row1, 6)
    o1 = v1a - theta * v1b
    o2 = v2a - theta * v2b
    length = (
        aa
        - 2.0 * theta * ab
        + theta * theta * bb
        - 2.0 * o1 * o1
        - 2.0 * o2 * o2
        + o1 * o1 * v1v1
        + 2.0 * o1 * o2 * v1v2
        + o2 * o2 * v2v2
    )
    r = 1.0 / jnp.sqrt(jnp.maximum(length, 0.0) + epsilon)
    return r, -r * theta, -r * o1 * inv, -r * o2


def fold(x):
    return jnp.sum(x.reshape(x.shape[0] // 8, 8, x.shape[1]), axis=0)


def row_from(sums):
    lane = lax.broadcasted_iota(jnp.int32, (1, 128), 1)
    row = jnp.zeros((1, 128), f32)
    for k, total in enumerate(sums):
        row = row + jnp.where(lane == k, jnp.sum(total), 0.0)
    return row


def keep_of(dims_ref, s, width):
    rows = lax.broadcasted_iota(jnp.int32, (width, width), 0)
    cols = lax.broadcasted_iota(jnp.int32, (width, width), 1)
    return (rows < dims_ref[0, s]) & (cols < dims_ref[1, s])


def start_kernel(dims_ref, psi_ref, out_ref):
    blocks, width = psi_ref.shape[0], psi_ref.shape[1]
    pieces, share = out_ref.shape[0], out_ref.shape[2]

    def body(s, carry):
        cols = lax.broadcasted_iota(jnp.int32, (share, width), 1) < dims_ref[1, s]
        ids = lax.broadcasted_iota(jnp.int32, (share, width), 0)
        for p in range(pieces):
            keep = (ids < dims_ref[0, s] - p * share) & cols
            x = jnp.where(keep, psi_ref[s, pl.ds(p * share, share)].astype(f32), 0.0)
            out_ref[p, s] = x.astype(bf16)
        return carry

    lax.fori_loop(0, blocks, body, 0)


def reduce_kernel(stage, arrived_ref, psi_ref, d_ref, *refs):
    if stage > 1:
        sig1_ref, v2_ref, refs = refs[0], refs[1], refs[2:]
    mine_ref, row_ref = refs
    pieces, blocks, share, width = arrived_ref.shape

    def body(s, acc):
        sig = arrived_ref[0, s].astype(f32)
        for p in range(1, pieces):
            sig = sig + arrived_ref[p, s].astype(f32)
        mine_ref[s] = sig
        psi = psi_ref[s].astype(f32)
        rd = 1.0 / d_ref[s].astype(f32)
        a = sig * rd
        if stage == 1:
            b = psi * rd
            terms = (psi * sig, psi * a, psi * b, a * a, a * b, b * b, psi * psi)
        else:
            v2 = v2_ref[s]
            b = v2 * rd
            terms = (
                v2 * sig,
                psi * a,
                psi * b,
                v2 * a,
                v2 * b,
                a * a,
                a * b,
                b * b,
                psi * v2,
                v2 * v2,
                psi * sig,
                v2 * sig1_ref[s],
            )
        return tuple(t + fold(x) for t, x in zip(acc, terms))

    acc = lax.fori_loop(0, blocks, body, (jnp.zeros((8, width), f32),) * (7 if stage == 1 else 12))
    row_ref[...] = row_from(acc)


def update_kernel(stage, entries, *refs):
    tots, refs = refs[:stage], refs[stage:]
    psi_ref, d_ref, sig1_ref, refs = refs[0], refs[1], refs[2], refs[3:]
    if stage > 1:
        sig2_ref, v2_ref, refs = refs[0], refs[1], refs[2:]
    v_ref, vb_ref, all_ref = refs[:3]
    pieces, blocks, share, width = all_ref.shape
    rows = [row_of(t, entries) for t in tots]
    if stage == 1:
        p, q, w = (x[0, 0] for x in second_weights(*rows))
    else:
        p, q, w, y = (x[0, 0] for x in third_weights(*rows))

    def body(s, acc):
        psi = psi_ref[s].astype(f32)
        rd = 1.0 / d_ref[s].astype(f32)
        sig1 = sig1_ref[s]
        if stage == 1:
            v = (p * sig1 + q * psi) * rd + w * psi
        else:
            sig2, v2 = sig2_ref[s], v2_ref[s]
            v = (p * sig2 + q * v2) * rd + w * psi + y * v2
            acc = acc[0] + fold(v * sig1), acc[1] + fold(v * sig2)
        v_ref[s] = v
        vb = v.astype(bf16)
        vb_ref[s] = vb
        for k in range(pieces):
            all_ref[k, s] = vb
        return acc

    acc = lax.fori_loop(0, blocks, body, (jnp.zeros((8, width), f32),) * (0 if stage == 1 else 2))
    if stage > 1:
        zero = jnp.zeros((8, width), f32)
        refs[3][...] = row_from([zero, zero, zero, *acc])


def dot(a, b, ca, cb):
    return lax.dot_general(a, b, (((ca,), (cb,)), ((), ())), preferred_element_type=f32)


def product_kernel(stage, *refs):
    conn_ref, dims_ref, far_ref, own_ref, near_ref = refs[:5]
    refs = refs[5:]
    if stage == 3:
        psi_ref, v2_ref, part_ref, refs = refs[0], refs[1], refs[2], refs[3:]
    left_ref, right_ref = refs[:2]
    if stage < 3:
        out_ref, vb_ref = refs[2:]
    else:
        env_ref, row_ref, vb_ref, acc_ref = refs[2:]
    step = pl.program_id(0)
    pieces, blocks, share, width = own_ref.shape
    terms, together = left_ref.shape[:2]

    @pl.when(step == 0)
    def _():
        def body(s, carry):
            for seg, ref in enumerate((far_ref, own_ref, near_ref)):
                vb_ref[seg * blocks + s] = ref[:, s].reshape(width, width)
            return carry

        lax.fori_loop(0, blocks, body, 0)
        if stage == 3:
            acc_ref[...] = jnp.zeros_like(acc_ref)

    halves = []
    for u in range(together):
        s = step * together + u
        halves.append([dot(left_ref[t, u], vb_ref[conn_ref[t, s]], 1, 0).astype(bf16) for t in range(terms)])
    for u in range(together):
        s = step * together + u
        side = jnp.concatenate([right_ref[t, u] for t in range(terms)], axis=1)
        total = dot(jnp.concatenate(halves[u], axis=1), side, 1, 1)
        if stage < 3:
            total = jnp.where(keep_of(dims_ref, s, width), total, 0.0).astype(bf16)
            out_ref[:, u] = total.reshape(pieces, share, width)
        else:
            own_t = vb_ref[blocks + s].T
            for t in range(terms):
                env_ref[t, u] = (dot(own_t, halves[u][t], 1, 0) * width ** (-0.5)).astype(bf16)
            sums = [acc_ref[k] for k in range(3)]
            for p in range(pieces):
                part = total[p * share : (p + 1) * share]
                for k, ref in enumerate((psi_ref, v2_ref, own_ref)):
                    sums[k] += fold(ref[p, s].astype(f32) * part)
            for k in range(3):
                acc_ref[k] = sums[k]
    if stage == 3:

        @pl.when(step == pl.num_programs(0) - 1)
        def _():
            row_ref[...] = row_from([acc_ref[k] for k in range(3)]) + part_ref[...]


def product(stage, conn, dims, groups, more, left, right):
    terms, blocks, width = left.shape[:3]
    pieces, _, share, _ = groups[0].shape
    together = 2
    smem = pl.BlockSpec(memory_space=pltpu.SMEM)
    vmem = pl.BlockSpec(memory_space=pltpu.VMEM)
    env_spec = pl.BlockSpec((terms, together, width, width), lambda s: (0, s, 0, 0))
    scratch = [pltpu.VMEM((3 * blocks, width, width), bf16)]
    if stage < 3:
        out_shape = jax.ShapeDtypeStruct((pieces, blocks, share, width), bf16)
        out_specs = pl.BlockSpec((pieces, together, share, width), lambda s: (0, s, 0, 0))
    else:
        out_shape = (jax.ShapeDtypeStruct(left.shape, bf16), jax.ShapeDtypeStruct((1, 128), f32))
        out_specs = (env_spec, pl.BlockSpec((1, 128), lambda s: (0, 0)))
        scratch.append(pltpu.VMEM((3, 8, width), f32))
    return pl.pallas_call(
        lambda *refs: product_kernel(stage, *refs),
        grid=(blocks // together,),
        in_specs=[smem, smem] + [vmem] * (3 + len(more)) + [env_spec, env_spec],
        out_specs=out_specs,
        out_shape=out_shape,
        scratch_shapes=scratch,
        name=f"product_{stage}",
        compiler_params=pltpu.CompilerParams(vmem_limit_bytes=32 << 20),
    )(conn, dims, *groups, *more, left, right)


def call_small(kernel, dims, arrays, out_shape, name):
    smem = pl.BlockSpec(memory_space=pltpu.SMEM)
    vmem = pl.BlockSpec(memory_space=pltpu.VMEM)
    return pl.pallas_call(
        kernel,
        in_specs=[smem] * len(dims) + [vmem] * len(arrays),
        out_specs=jax.tree.map(lambda _: vmem, out_shape),
        out_shape=out_shape,
        name=name,
        compiler_params=pltpu.CompilerParams(vmem_limit_bytes=16 << 20),
    )(*dims, *arrays)


def last_kernel(entries, tot1, tot2, tot3, out_ref):
    r1, r2, r3 = (row_of(t, entries) for t in (tot1, tot2, tot3))
    inv = first_scale(r1)
    values = (
        (inv * inv * one(r1, 0), inv * one(r2, 10), inv * one(r3, 0)),
        (inv * one(r2, 11), one(r2, 0), one(r3, 1)),
        (inv * one(r3, 3), one(r3, 4), one(r3, 2)),
    )
    row = lax.broadcasted_iota(jnp.int32, (3, 3), 0)
    col = lax.broadcasted_iota(jnp.int32, (3, 3), 1)
    out = jnp.zeros((3, 3), f32)
    for i in range(3):
        for j in range(3):
            out = jnp.where((row == i) & (col == j), values[i][j], out)
    out_ref[...] = out


def on_device(psi_start, left_env, right_env, connect, sector_dims, precond):
    blocks, width = psi_start.shape[:2]
    devices = lax.axis_size("sector")
    pieces = lax.axis_size("term")
    share = width // pieces
    entries = float(blocks * devices * width * width)
    everyone = ("term", "sector")
    row = jax.ShapeDtypeStruct((1, 128), f32)
    cut = jax.ShapeDtypeStruct((pieces, blocks, share, width), bf16)
    part = jax.ShapeDtypeStruct((blocks, share, width), f32)
    part_b = jax.ShapeDtypeStruct((blocks, share, width), bf16)
    place = lax.axis_index("sector")
    conn = connect - (place * blocks - blocks)
    turned = (2 - conn // blocks) * blocks + conn % blocks
    conn = jnp.where(place % 2 == 1, turned, conn)
    args = (left_env, right_env)

    def far(mine):
        return to_everyone(swapped(mine, 1), "term")

    def near(block):
        return swapped(block, 0)

    def exchange(x):
        return lax.all_to_all(x, "term", 0, 0, tiled=True)

    def reduced(stage, partial, *shares):
        return call_small(
            lambda *refs: reduce_kernel(stage, *refs), [], [exchange(partial), *shares], (part, row), f"reduce_{stage}"
        )

    def updated(stage, tots, *shares):
        out = (part, part_b, cut) + ((row,) if stage > 1 else ())
        v, vb, every, *more = call_small(
            lambda *refs: update_kernel(stage, entries, *refs), [], [*tots, *shares], out, f"update_{stage}"
        )
        own = exchange(every)
        return v, (far(vb), own, near(own)), more

    psi = call_small(start_kernel, [sector_dims], [psi_start], cut, "start")
    term = lax.axis_index("term")
    psi_share = lax.dynamic_index_in_dim(psi, term, 0, keepdims=False)
    d_share = lax.dynamic_slice_in_dim(precond, term * share, share, 1)

    partial = product(1, conn, sector_dims, (far(psi_share), psi, near(psi)), (), *args)
    sig1, row1 = reduced(1, partial, psi_share, d_share)
    tot1 = to_everyone(row1[0], everyone)
    v2, groups2, _ = updated(1, (tot1,), psi_share, d_share, sig1)

    partial = product(2, conn, sector_dims, groups2, (), *args)
    sig2, row2 = reduced(2, partial, psi_share, d_share, sig1, v2)
    tot2 = to_everyone(row2[0], everyone)
    v3, groups3, (more,) = updated(2, (tot1, tot2), psi_share, d_share, sig1, sig2, v2)

    env, row3 = product(3, conn, sector_dims, groups3, (psi, groups2[1], more), *args)
    tot3 = to_everyone(row3[0], everyone)
    projected = call_small(
        lambda *refs: last_kernel(entries, *refs), [], [tot1, tot2, tot3], jax.ShapeDtypeStruct((3, 3), f32), "last"
    )
    return (projected, v3, env)


def solution(mesh):
    placed = (
        P("sector", None, None),
        P("term", "sector", None, None),
        P("term", "sector", None, None),
        P("term", "sector"),
        P(None, "sector"),
        P("sector", None, None),
    )
    return jax.shard_map(
        on_device,
        mesh=mesh,
        in_specs=placed,
        out_specs=(P(), P("sector", "term", None), P("term", "sector", None, None)),
        check_vma=False,
    )
```

```python
import jax
import jax.numpy as jnp
from jax import lax
from jax.experimental import pallas as pl
from jax.experimental.pallas import tpu as pltpu
from jax.sharding import PartitionSpec as P

epsilon = 1e-06
f32 = jnp.float32
bf16 = jnp.bfloat16


def to_everyone(x, axis):
    devices = lax.axis_size(axis)
    return lax.all_to_all(jnp.broadcast_to(x[None], (devices, *x.shape)), axis, 0, 0, tiled=True)


def swapped(block, first):
    pairs = [(i, i + 1) for i in range(first, lax.axis_size("sector") - 1, 2)]
    return lax.ppermute(block, "sector", pairs + [(j, i) for i, j in pairs])


def row_of(total_ref, entries):
    return jnp.sum(total_ref[...], axis=0, keepdims=True) * (1.0 / entries)


def one(row, k):
    return row[:, k : k + 1]


def first_scale(row1):
    return 1.0 / jnp.sqrt(one(row1, 6) + epsilon)


def second_weights(row1):
    inv = first_scale(row1)
    theta, a, b, aa, ab, bb, vv = (inv * inv * one(row1, k) for k in range(7))
    o = a - theta * b
    length = aa + theta * theta * bb + o * o * vv - 2.0 * theta * ab - 2.0 * o * a + 2.0 * theta * o * b
    r = 1.0 / jnp.sqrt(jnp.maximum(length, 0.0) + epsilon)
    return r * inv, -r * theta * inv, -r * o * inv


def third_weights(row1, row2):
    inv = first_scale(row1)
    theta = one(row2, 0)
    v1a = inv * one(row2, 1)
    v1b = inv * one(row2, 2)
    v2a = one(row2, 3)
    v2b = one(row2, 4)
    aa = one(row2, 5)
    ab = one(row2, 6)
    bb = one(row2, 7)
    v1v2 = inv * one(row2, 8)
    v2v2 = one(row2, 9)
    v1v1 = inv * inv * one(row1, 6)
    o1 = v1a - theta * v1b
    o2 = v2a - theta * v2b
    length = (
        aa
        - 2.0 * theta * ab
        + theta * theta * bb
        - 2.0 * o1 * o1
        - 2.0 * o2 * o2
        + o1 * o1 * v1v1
        + 2.0 * o1 * o2 * v1v2
        + o2 * o2 * v2v2
    )
    r = 1.0 / jnp.sqrt(jnp.maximum(length, 0.0) + epsilon)
    return r, -r * theta, -r * o1 * inv, -r * o2


def fold(x):
    return jnp.sum(x.reshape(x.shape[0] // 8, 8, x.shape[1]), axis=0)


def row_from(sums):
    lane = lax.broadcasted_iota(jnp.int32, (1, 128), 1)
    row = jnp.zeros((1, 128), f32)
    for k, total in enumerate(sums):
        row = row + jnp.where(lane == k, jnp.sum(total), 0.0)
    return row


def keep_of(dims_ref, s, width):
    rows = lax.broadcasted_iota(jnp.int32, (width, width), 0)
    cols = lax.broadcasted_iota(jnp.int32, (width, width), 1)
    return (rows < dims_ref[0, s]) & (cols < dims_ref[1, s])


def masked(x, dims_ref, s, first):
    rows = lax.broadcasted_iota(jnp.int32, x.shape, 0)
    cols = lax.broadcasted_iota(jnp.int32, x.shape, 1)
    keep = (rows < dims_ref[0, s] - first) & (cols < dims_ref[1, s])
    return jnp.where(keep, x.astype(f32), 0.0).astype(bf16)


def share_kernel(dims_ref, psi_ref, d_ref, shares_ref, buf_ref, sem):
    blocks, share = buf_ref.shape[1:3]
    first = lax.axis_index("term") * share
    mine = pl.ds(pl.multiple_of(first, share), share)
    copies = [pltpu.make_async_copy(x.at[:, mine], buf_ref.at[k], sem.at[k]) for k, x in enumerate((psi_ref, d_ref))]
    for copy in copies:
        copy.start()
    for copy in copies:
        copy.wait()
    for s in range(blocks):
        buf_ref[0, s] = masked(buf_ref[0, s], dims_ref, s, first)
    copy = pltpu.make_async_copy(buf_ref, shares_ref, sem.at[2])
    copy.start()
    copy.wait()


def start_kernel(dims_ref, psi_ref, out_ref):
    pieces, blocks, share = out_ref.shape[:3]

    def body(s, carry):
        for p in range(pieces):
            out_ref[p, s] = masked(psi_ref[s, pl.ds(p * share, share)], dims_ref, s, p * share)
        return carry

    lax.fori_loop(0, blocks, body, 0)


def reduce_kernel(stage, arrived_ref, shares_ref, *refs):
    if stage > 1:
        sig1_ref, v2_ref, refs = refs[0], refs[1], refs[2:]
    mine_ref, send_ref, row_ref, sem = refs
    pieces, blocks, share, width = arrived_ref.shape

    def body(s, acc):
        sig = arrived_ref[0, s].astype(f32)
        for p in range(1, pieces):
            sig = sig + arrived_ref[p, s].astype(f32)
        mine_ref[s] = sig
        psi = shares_ref[0, s].astype(f32)
        rd = 1.0 / shares_ref[1, s].astype(f32)
        a = sig * rd
        if stage == 1:
            b = psi * rd
            terms = (psi * sig, psi * a, psi * b, a * a, a * b, b * b, psi * psi)
        else:
            v2 = v2_ref[s]
            b = v2 * rd
            terms = (
                v2 * sig,
                psi * a,
                psi * b,
                v2 * a,
                v2 * b,
                a * a,
                a * b,
                b * b,
                psi * v2,
                v2 * v2,
                psi * sig,
                v2 * sig1_ref[s],
            )
        return tuple(t + fold(x) for t, x in zip(acc, terms))

    acc = lax.fori_loop(0, blocks, body, (jnp.zeros((8, width), f32),) * (7 if stage == 1 else 12))
    copy = pltpu.make_async_copy(mine_ref, send_ref, sem)
    copy.start()
    row_ref[...] = row_from(acc)
    copy.wait()


def update_kernel(stage, entries, *refs):
    tots, refs = refs[:stage], refs[stage:]
    per = 2 if stage == 1 else 4
    groups, refs = (refs[:per], refs[per : 2 * per]), refs[2 * per :]
    v_refs, refs = refs[:2], refs[2:]
    if stage > 1:
        row_ref, refs = refs[0], refs[1:]
    all_ref, buf_ref, sem = refs
    pieces, _, blocks, share, width = all_ref.shape
    rows = [row_of(t, entries) for t in tots]
    if stage == 1:
        p, q, w = (x[0, 0] for x in second_weights(*rows))
    else:
        p, q, w, y = (x[0, 0] for x in third_weights(*rows))
    copies = []
    for g in range(2):

        def body(s, acc, g=g):
            psi = groups[g][0][0, s].astype(f32)
            rd = 1.0 / groups[g][0][1, s].astype(f32)
            sig1 = groups[g][1][s]
            if stage == 1:
                v = (p * sig1 + q * psi) * rd + w * psi
            else:
                sig2, v2 = groups[g][2][s], groups[g][3][s]
                v = (p * sig2 + q * v2) * rd + w * psi + y * v2
                acc = acc[0] + fold(v * sig1), acc[1] + fold(v * sig2)
            v_refs[g][s] = v
            buf_ref[g, s] = v.astype(bf16)
            return acc

        acc = lax.fori_loop(0, blocks, body, (jnp.zeros((8, width), f32),) * (0 if stage == 1 else 2))
        if stage > 1 and g == 0:
            zero = jnp.zeros((8, width), f32)
            row_ref[...] = row_from([zero, zero, zero, *acc])
        for k in range(pieces):
            copies.append(pltpu.make_async_copy(buf_ref.at[g], all_ref.at[k, g], sem.at[g, k]))
            copies[-1].start()
    for copy in copies:
        copy.wait()


def dot(a, b, ca, cb):
    return lax.dot_general(a, b, (((ca,), (cb,)), ((), ())), preferred_element_type=f32)


together = 2


def product_kernel(stage, *refs):
    conn_ref, dims_ref, groups, refs = refs[0], refs[1], refs[2 : 4 + (stage == 1)], refs[4 + (stage == 1) :]
    if stage == 1:
        far_ref, own_ref, near_ref = groups
    else:
        own_ref, far_ref, near_ref = groups[0].at[:, 0], groups[0].at[:, 1], groups[1]
    if stage == 3:
        psi_ref, v2_ref, part_ref, refs = refs[0], refs[1], refs[2], refs[3:]
    sources = refs[: 1 if stage == 4 else 2]
    refs = refs[len(sources) :]
    out_ref, vb_ref = refs[:2]
    sides = sources
    incoming = []
    if stage == 1:
        right_ref, in_sem = refs[2:4]
        for g in range(right_ref.shape[1] // together):
            at = pl.ds(g * together, together)
            incoming.append(pltpu.make_async_copy(sources[1].at[:, at], right_ref.at[:, at], in_sem.at[g]))
        sides = (sources[0], right_ref)
    for copy in incoming:
        copy.start()
    if stage != 3:
        buf_ref, out_sem = refs[-2:]
    pieces, blocks, share, width = own_ref.shape
    terms = sources[0].shape[0]
    steps = blocks // together
    def body(s, carry):
        for seg, ref in enumerate((far_ref, own_ref, near_ref)):
            vb_ref[seg * blocks + s] = ref[:, s].reshape(width, width)
        return carry

    lax.fori_loop(0, blocks, body, 0)
    outgoing = []
    sums = [jnp.zeros((8, width), f32)] * 3
    for g in range(steps):
        here = range(g * together, (g + 1) * together)
        halves = {
            s: [dot(sides[0][t, s], vb_ref[conn_ref[t, s]], 1, 0).astype(bf16) for t in range(terms)] for s in here
        }
        if incoming:
            incoming[g].wait()
        for s in here:
            if stage == 4:
                own_t = vb_ref[blocks + s].T
                for t in range(terms):
                    buf_ref[t, s] = (dot(own_t, halves[s][t], 1, 0) * width ** (-0.5)).astype(bf16)
                continue
            side = jnp.concatenate([sides[1][t, s] for t in range(terms)], axis=1)
            total = dot(jnp.concatenate(halves[s], axis=1), side, 1, 1)
            if stage < 3:
                total = jnp.where(keep_of(dims_ref, s, width), total, 0.0).astype(bf16)
                buf_ref[:, s] = total.reshape(pieces, share, width)
            else:
                for p in range(pieces):
                    part = total[p * share : (p + 1) * share]
                    for k, x in enumerate((psi_ref[p, s], v2_ref[p, 0, s], own_ref[p, s])):
                        sums[k] = sums[k] + fold(x.astype(f32) * part)
        if stage != 3:
            at = pl.ds(g * together, together)
            outgoing.append(pltpu.make_async_copy(buf_ref.at[:, at], out_ref.at[:, at], out_sem.at[g]))
            outgoing[-1].start()
    for copy in outgoing:
        copy.wait()
    if stage == 3:
        out_ref[...] = row_from(sums) + part_ref[...]


def product(stage, conn, dims, groups, more, *sides):
    terms, blocks, width = sides[0].shape[:3]
    pieces, share = groups[-1].shape[0], groups[-1].shape[2]
    smem = pl.BlockSpec(memory_space=pltpu.SMEM)
    vmem = pl.BlockSpec(memory_space=pltpu.VMEM)
    hbm = pl.BlockSpec(memory_space=pltpu.HBM)
    steps = blocks // together
    scratch = [pltpu.VMEM((3 * blocks, width, width), bf16)]
    if stage == 1:
        scratch += [pltpu.VMEM(sides[1].shape, bf16), pltpu.SemaphoreType.DMA((steps,))]
    if stage == 3:
        out_shape, out_specs = jax.ShapeDtypeStruct((1, 128), f32), vmem
    else:
        shape = sides[0].shape if stage == 4 else (pieces, blocks, share, width)
        out_shape, out_specs = pltpu.HBM(shape, bf16), hbm
        scratch += [pltpu.VMEM(shape, bf16), pltpu.SemaphoreType.DMA((steps,))]
    return pl.pallas_call(
        lambda *refs: product_kernel(stage, *refs),
        in_specs=[smem, smem] + [vmem] * (len(groups) + len(more) + len(sides) - (stage == 1)) + [hbm] * (stage == 1),
        out_specs=out_specs,
        out_shape=out_shape,
        scratch_shapes=scratch,
        name=f"product_{stage}",
        compiler_params=pltpu.CompilerParams(vmem_limit_bytes=12 << 20),
    )(conn, dims, *groups, *more, *sides)


def keep_kernel(here_ref, there_ref, sem):
    copies = [pltpu.make_async_copy(here_ref.at[t], there_ref.at[t], sem.at[t]) for t in range(here_ref.shape[0])]
    for copy in copies:
        copy.start()
    for copy in copies:
        copy.wait()


def kept(x):
    return pl.pallas_call(
        keep_kernel,
        in_specs=[pl.BlockSpec(memory_space=pltpu.HBM)],
        out_specs=pl.BlockSpec(memory_space=pltpu.VMEM),
        out_shape=pltpu.VMEM(x.shape, x.dtype),
        scratch_shapes=[pltpu.SemaphoreType.DMA((x.shape[0],))],
        name="keep",
        compiler_params=pltpu.CompilerParams(vmem_limit_bytes=1 << 20),
    )(pltpu.with_memory_space_constraint(x, pltpu.HBM))


def call_small(kernel, dims, arrays, out_shape, name, sent=None, scratch=()):
    smem = pl.BlockSpec(memory_space=pltpu.SMEM)
    vmem = pl.BlockSpec(memory_space=pltpu.VMEM)
    out_specs = jax.tree.map(lambda _: vmem, out_shape)
    if sent is not None:
        out_specs = tuple(pl.BlockSpec(memory_space=pltpu.HBM) if k == sent else x for k, x in enumerate(out_specs))
    return pl.pallas_call(
        kernel,
        in_specs=[smem] * len(dims) + [vmem] * len(arrays),
        out_specs=out_specs,
        out_shape=out_shape,
        scratch_shapes=scratch,
        name=name,
        compiler_params=pltpu.CompilerParams(vmem_limit_bytes=8 << 20),
    )(*dims, *arrays)


def last_kernel(entries, tot1, tot2, tot3, out_ref):
    r1, r2, r3 = (row_of(t, entries) for t in (tot1, tot2, tot3))
    inv = first_scale(r1)
    values = (
        (inv * inv * one(r1, 0), inv * one(r2, 10), inv * one(r3, 0)),
        (inv * one(r2, 11), one(r2, 0), one(r3, 1)),
        (inv * one(r3, 3), one(r3, 4), one(r3, 2)),
    )
    row = lax.broadcasted_iota(jnp.int32, (3, 3), 0)
    col = lax.broadcasted_iota(jnp.int32, (3, 3), 1)
    out = jnp.zeros((3, 3), f32)
    for i in range(3):
        for j in range(3):
            out = jnp.where((row == i) & (col == j), values[i][j], out)
    out_ref[...] = out


def on_device(psi_start, left_env, right_env, connect, sector_dims, precond):
    blocks, width = psi_start.shape[:2]
    devices = lax.axis_size("sector")
    pieces = lax.axis_size("term")
    share = width // pieces
    entries = float(blocks * devices * width * width)
    everyone = ("term", "sector")
    row = jax.ShapeDtypeStruct((1, 128), f32)
    cut = jax.ShapeDtypeStruct((pieces, blocks, share, width), bf16)
    part = jax.ShapeDtypeStruct((blocks, share, width), f32)
    place = lax.axis_index("sector")
    conn = connect - (place * blocks - blocks)
    turned = (2 - conn // blocks) * blocks + conn % blocks
    conn = jnp.where(place % 2 == 1, turned, conn)

    def exchange(x):
        return lax.all_to_all(x, "term", 0, 0, tiled=True)

    def reduced(stage, partial, *shares):
        mine, sent, sums = call_small(
            lambda *refs: reduce_kernel(stage, *refs),
            [],
            [exchange(partial), *shares],
            (part, pltpu.HBM(part.shape, f32), row),
            f"reduce_{stage}",
            1,
            [pltpu.SemaphoreType.DMA],
        )
        sums = jnp.broadcast_to(sums, (pieces * devices, 128))
        sums, sent = lax.optimization_barrier((sums, sent))
        return (mine, swapped(sent, 1)), lax.all_to_all(sums, everyone, 0, 0, tiled=True)

    def updated(stage, tots, own, far):
        out = (part, part) + ((row,) if stage > 1 else ())
        every = pltpu.HBM((pieces, 2, blocks, share, width), bf16)
        v, v_far, *more, every = call_small(
            lambda *refs: update_kernel(stage, entries, *refs),
            [],
            [*tots, *own, *far],
            (*out, every),
            f"update_{stage}",
            len(out),
            [pltpu.VMEM((2, blocks, share, width), bf16), pltpu.SemaphoreType.DMA((2, pieces))],
        )
        both = exchange(every)
        return (v, v_far), (both, swapped(both[:, 0], 0)), more

    hbm = pl.BlockSpec(memory_space=pltpu.HBM)
    shares = pl.pallas_call(
        share_kernel,
        in_specs=[pl.BlockSpec(memory_space=pltpu.SMEM), hbm, hbm],
        out_specs=hbm,
        out_shape=pltpu.HBM((2, blocks, share, width), bf16),
        scratch_shapes=[pltpu.VMEM((2, blocks, share, width), bf16), pltpu.SemaphoreType.DMA((3,))],
        name="share",
        compiler_params=pltpu.CompilerParams(vmem_limit_bytes=4 << 20),
    )(
        sector_dims,
        pltpu.with_memory_space_constraint(psi_start, pltpu.HBM),
        pltpu.with_memory_space_constraint(precond, pltpu.HBM),
    )
    psi = call_small(start_kernel, [sector_dims], [psi_start], cut, "start")
    far = swapped(shares, 1)
    left_env = kept(left_env)

    groups = (to_everyone(far[0], "term"), psi, swapped(psi, 0))
    partial = product(1, conn, sector_dims, groups, (), left_env, pltpu.with_memory_space_constraint(right_env, pltpu.HBM))
    sig1, tot1 = reduced(1, partial, shares)
    v2, groups2, _ = updated(1, (tot1,), (shares, sig1[0]), (far, sig1[1]))

    partial = product(2, conn, sector_dims, groups2, (), left_env, right_env)
    sig2, tot2 = reduced(2, partial, shares, sig1[0], v2[0])
    v3, groups3, (more,) = updated(2, (tot1, tot2), (shares, sig1[0], sig2[0], v2[0]), (far, sig1[1], sig2[1], v2[1]))

    row3 = product(3, conn, sector_dims, groups3, (psi, groups2[0], more), left_env, right_env)
    tot3 = to_everyone(row3[0], everyone)
    env = product(4, conn, sector_dims, groups3, (), left_env)
    projected = call_small(
        lambda *refs: last_kernel(entries, *refs), [], [tot1, tot2, tot3], jax.ShapeDtypeStruct((3, 3), f32), "last"
    )
    return (projected, v3[0], env)


def solution(mesh):
    placed = (
        P("sector", None, None),
        P("term", "sector", None, None),
        P("term", "sector", None, None),
        P("term", "sector"),
        P(None, "sector"),
        P("sector", None, None),
    )
    return jax.shard_map(
        on_device,
        mesh=mesh,
        in_specs=placed,
        out_specs=(P(), P("sector", "term", None), P("term", "sector", None, None)),
        check_vma=False,
    )
```

```python
import jax
import jax.numpy as jnp
from jax import lax
from jax.experimental import pallas as pl
from jax.experimental.pallas import tpu as pltpu
from jax.sharding import PartitionSpec as P

epsilon = 1e-06
f32 = jnp.float32
bf16 = jnp.bfloat16


def to_everyone(x, axis):
    devices = lax.axis_size(axis)
    return lax.all_to_all(jnp.broadcast_to(x[None], (devices, *x.shape)), axis, 0, 0, tiled=True)


def swapped(block, first):
    pairs = [(i, i + 1) for i in range(first, lax.axis_size("sector") - 1, 2)]
    return lax.ppermute(block, "sector", pairs + [(j, i) for i, j in pairs])


def row_of(total_ref, entries):
    return jnp.sum(total_ref[...], axis=0, keepdims=True) * (1.0 / entries)


def one(row, k):
    return row[:, k : k + 1]


def first_scale(row1):
    return 1.0 / jnp.sqrt(one(row1, 6) + epsilon)


def second_weights(row1):
    inv = first_scale(row1)
    theta, a, b, aa, ab, bb, vv = (inv * inv * one(row1, k) for k in range(7))
    o = a - theta * b
    length = aa + theta * theta * bb + o * o * vv - 2.0 * theta * ab - 2.0 * o * a + 2.0 * theta * o * b
    r = 1.0 / jnp.sqrt(jnp.maximum(length, 0.0) + epsilon)
    return r * inv, -r * theta * inv, -r * o * inv


def third_weights(row1, row2):
    inv = first_scale(row1)
    theta = one(row2, 0)
    v1a = inv * one(row2, 1)
    v1b = inv * one(row2, 2)
    v2a = one(row2, 3)
    v2b = one(row2, 4)
    aa = one(row2, 5)
    ab = one(row2, 6)
    bb = one(row2, 7)
    v1v2 = inv * one(row2, 8)
    v2v2 = one(row2, 9)
    v1v1 = inv * inv * one(row1, 6)
    o1 = v1a - theta * v1b
    o2 = v2a - theta * v2b
    length = (
        aa
        - 2.0 * theta * ab
        + theta * theta * bb
        - 2.0 * o1 * o1
        - 2.0 * o2 * o2
        + o1 * o1 * v1v1
        + 2.0 * o1 * o2 * v1v2
        + o2 * o2 * v2v2
    )
    r = 1.0 / jnp.sqrt(jnp.maximum(length, 0.0) + epsilon)
    return r, -r * theta, -r * o1 * inv, -r * o2


def fold(x):
    return jnp.sum(x.reshape(x.shape[0] // 8, 8, x.shape[1]), axis=0)


def row_from(sums):
    lane = lax.broadcasted_iota(jnp.int32, (1, 128), 1)
    row = jnp.zeros((1, 128), f32)
    for k, total in enumerate(sums):
        row = row + jnp.where(lane == k, jnp.sum(total), 0.0)
    return row


def keep_of(dims_ref, s, width):
    rows = lax.broadcasted_iota(jnp.int32, (width, width), 0)
    cols = lax.broadcasted_iota(jnp.int32, (width, width), 1)
    return (rows < dims_ref[0, s]) & (cols < dims_ref[1, s])


def masked(x, dims_ref, s, first):
    rows = lax.broadcasted_iota(jnp.int32, x.shape, 0)
    cols = lax.broadcasted_iota(jnp.int32, x.shape, 1)
    keep = (rows < dims_ref[0, s] - first) & (cols < dims_ref[1, s])
    return jnp.where(keep, x.astype(f32), 0.0).astype(bf16)


def share_kernel(dims_ref, psi_ref, d_ref, shares_ref, buf_ref, sem):
    blocks, share = buf_ref.shape[1:3]
    first = lax.axis_index("term") * share
    mine = pl.ds(pl.multiple_of(first, share), share)
    copies = [pltpu.make_async_copy(x.at[:, mine], buf_ref.at[k], sem.at[k]) for k, x in enumerate((psi_ref, d_ref))]
    for copy in copies:
        copy.start()
    for copy in copies:
        copy.wait()
    for s in range(blocks):
        buf_ref[0, s] = masked(buf_ref[0, s], dims_ref, s, first)
    copy = pltpu.make_async_copy(buf_ref, shares_ref, sem.at[2])
    copy.start()
    copy.wait()


def start_kernel(dims_ref, psi_ref, out_ref):
    pieces, blocks, share = out_ref.shape[:3]

    def body(s, carry):
        for p in range(pieces):
            out_ref[p, s] = masked(psi_ref[s, pl.ds(p * share, share)], dims_ref, s, p * share)
        return carry

    lax.fori_loop(0, blocks, body, 0)


def reduce_kernel(stage, arrived_ref, shares_ref, *refs):
    if stage > 1:
        sig1_ref, v2_ref, refs = refs[0], refs[1], refs[2:]
    mine_ref, send_ref, row_ref, sem = refs
    pieces, blocks, share, width = arrived_ref.shape

    def body(s, acc):
        sig = arrived_ref[0, s].astype(f32)
        for p in range(1, pieces):
            sig = sig + arrived_ref[p, s].astype(f32)
        mine_ref[s] = sig
        psi = shares_ref[0, s].astype(f32)
        rd = 1.0 / shares_ref[1, s].astype(f32)
        a = sig * rd
        if stage == 1:
            b = psi * rd
            terms = (psi * sig, psi * a, psi * b, a * a, a * b, b * b, psi * psi)
        else:
            v2 = v2_ref[s]
            b = v2 * rd
            terms = (
                v2 * sig,
                psi * a,
                psi * b,
                v2 * a,
                v2 * b,
                a * a,
                a * b,
                b * b,
                psi * v2,
                v2 * v2,
                psi * sig,
                v2 * sig1_ref[s],
            )
        return tuple(t + fold(x) for t, x in zip(acc, terms))

    acc = lax.fori_loop(0, blocks, body, (jnp.zeros((8, width), f32),) * (7 if stage == 1 else 12))
    copy = pltpu.make_async_copy(mine_ref, send_ref, sem)
    copy.start()
    row_ref[...] = row_from(acc)
    copy.wait()


def update_kernel(stage, entries, *refs):
    tots, refs = refs[:stage], refs[stage:]
    per = 2 if stage == 1 else 4
    groups, refs = (refs[:per], refs[per : 2 * per]), refs[2 * per :]
    v_refs, refs = refs[:2], refs[2:]
    if stage > 1:
        row_ref, refs = refs[0], refs[1:]
    all_ref, buf_ref, sem = refs
    pieces, _, blocks, share, width = all_ref.shape
    rows = [row_of(t, entries) for t in tots]
    if stage == 1:
        p, q, w = (x[0, 0] for x in second_weights(*rows))
    else:
        p, q, w, y = (x[0, 0] for x in third_weights(*rows))
    copies = []
    for g in range(2):

        def body(s, acc, g=g):
            psi = groups[g][0][0, s].astype(f32)
            rd = 1.0 / groups[g][0][1, s].astype(f32)
            sig1 = groups[g][1][s]
            if stage == 1:
                v = (p * sig1 + q * psi) * rd + w * psi
            else:
                sig2, v2 = groups[g][2][s], groups[g][3][s]
                v = (p * sig2 + q * v2) * rd + w * psi + y * v2
                acc = acc[0] + fold(v * sig1), acc[1] + fold(v * sig2)
            v_refs[g][s] = v
            buf_ref[g, s] = v.astype(bf16)
            return acc

        acc = lax.fori_loop(0, blocks, body, (jnp.zeros((8, width), f32),) * (0 if stage == 1 else 2))
        if stage > 1 and g == 0:
            zero = jnp.zeros((8, width), f32)
            row_ref[...] = row_from([zero, zero, zero, *acc])
        for k in range(pieces):
            copies.append(pltpu.make_async_copy(buf_ref.at[g], all_ref.at[k, g], sem.at[g, k]))
            copies[-1].start()
    for copy in copies:
        copy.wait()


def dot(a, b, ca, cb):
    return lax.dot_general(a, b, (((ca,), (cb,)), ((), ())), preferred_element_type=f32)


together = 2


def product_kernel(stage, *refs):
    conn_ref, dims_ref, groups, refs = refs[0], refs[1], refs[2 : 4 + (stage == 1)], refs[4 + (stage == 1) :]
    if stage == 1:
        far_ref, own_ref, near_ref = groups
    else:
        own_ref, far_ref, near_ref = groups[0].at[:, 0], groups[0].at[:, 1], groups[1]
    if stage == 3:
        psi_ref, v2_ref, part_ref, refs = refs[0], refs[1], refs[2], refs[3:]
    sources = refs[: 1 if stage == 4 else 2]
    refs = refs[len(sources) :]
    out_ref, vb_ref = refs[:2]
    sides = sources
    incoming = []
    if stage == 1:
        sides, in_sem = refs[2:4], refs[4]
        for g in range(sources[0].shape[1] // together):
            at = pl.ds(g * together, together)
            incoming += [
                pltpu.make_async_copy(x.at[:, at], y.at[:, at], in_sem.at[k, g]) for k, (x, y) in enumerate(zip(sources, sides))
            ]
    for copy in incoming:
        copy.start()
    if stage != 3:
        buf_ref, out_sem = refs[-2:]
    pieces, blocks, share, width = own_ref.shape
    terms = sources[0].shape[0]
    steps = blocks // together
    def body(s, carry):
        for seg, ref in enumerate((far_ref, own_ref, near_ref)):
            vb_ref[seg * blocks + s] = ref[:, s].reshape(width, width)
        return carry

    lax.fori_loop(0, blocks, body, 0)
    outgoing = []
    sums = [jnp.zeros((8, width), f32)] * 3
    for g in range(steps):
        here = range(g * together, (g + 1) * together)
        for copy in incoming[2 * g : 2 * g + 2]:
            copy.wait()
        halves = {
            s: [dot(sides[0][t, s], vb_ref[conn_ref[t, s]], 1, 0).astype(bf16) for t in range(terms)] for s in here
        }
        for s in here:
            if stage == 4:
                own_t = vb_ref[blocks + s].T
                for t in range(terms):
                    buf_ref[t, s] = (dot(own_t, halves[s][t], 1, 0) * width ** (-0.5)).astype(bf16)
                continue
            side = jnp.concatenate([sides[1][t, s] for t in range(terms)], axis=1)
            total = dot(jnp.concatenate(halves[s], axis=1), side, 1, 1)
            if stage < 3:
                total = jnp.where(keep_of(dims_ref, s, width), total, 0.0).astype(bf16)
                buf_ref[:, s] = total.reshape(pieces, share, width)
            else:
                for p in range(pieces):
                    part = total[p * share : (p + 1) * share]
                    for k, x in enumerate((psi_ref[p, s], v2_ref[p, 0, s], own_ref[p, s])):
                        sums[k] = sums[k] + fold(x.astype(f32) * part)
        if stage != 3:
            at = pl.ds(g * together, together)
            outgoing.append(pltpu.make_async_copy(buf_ref.at[:, at], out_ref.at[:, at], out_sem.at[g]))
            outgoing[-1].start()
    for copy in outgoing:
        copy.wait()
    if stage == 3:
        out_ref[...] = row_from(sums) + part_ref[...]


def product(stage, conn, dims, groups, more, *sides):
    terms, blocks, width = sides[0].shape[:3]
    pieces, share = groups[-1].shape[0], groups[-1].shape[2]
    smem = pl.BlockSpec(memory_space=pltpu.SMEM)
    vmem = pl.BlockSpec(memory_space=pltpu.VMEM)
    hbm = pl.BlockSpec(memory_space=pltpu.HBM)
    steps = blocks // together
    scratch = [pltpu.VMEM((3 * blocks, width, width), bf16)]
    if stage == 1:
        scratch += [pltpu.VMEM(x.shape, bf16) for x in sides]
        scratch.append(pltpu.SemaphoreType.DMA((2, steps)))
    if stage == 3:
        out_shape, out_specs = jax.ShapeDtypeStruct((1, 128), f32), vmem
    else:
        shape = sides[0].shape if stage == 4 else (pieces, blocks, share, width)
        out_shape, out_specs = pltpu.HBM(shape, bf16), hbm
        scratch += [pltpu.VMEM(shape, bf16), pltpu.SemaphoreType.DMA((steps,))]
    return pl.pallas_call(
        lambda *refs: product_kernel(stage, *refs),
        in_specs=[smem, smem] + [vmem] * (len(groups) + len(more)) + [hbm if stage == 1 else vmem] * len(sides),
        out_specs=out_specs,
        out_shape=out_shape,
        scratch_shapes=scratch,
        name=f"product_{stage}",
        compiler_params=pltpu.CompilerParams(vmem_limit_bytes=12 << 20),
    )(conn, dims, *groups, *more, *sides)


def keep_kernel(here_ref, there_ref, sem):
    copies = [pltpu.make_async_copy(here_ref.at[t], there_ref.at[t], sem.at[t]) for t in range(here_ref.shape[0])]
    for copy in copies:
        copy.start()
    for copy in copies:
        copy.wait()


def kept(x):
    return pl.pallas_call(
        keep_kernel,
        in_specs=[pl.BlockSpec(memory_space=pltpu.HBM)],
        out_specs=pl.BlockSpec(memory_space=pltpu.VMEM),
        out_shape=pltpu.VMEM(x.shape, x.dtype),
        scratch_shapes=[pltpu.SemaphoreType.DMA((x.shape[0],))],
        name="keep",
        compiler_params=pltpu.CompilerParams(vmem_limit_bytes=1 << 20),
    )(pltpu.with_memory_space_constraint(x, pltpu.HBM))


def call_small(kernel, dims, arrays, out_shape, name, sent=None, scratch=()):
    smem = pl.BlockSpec(memory_space=pltpu.SMEM)
    vmem = pl.BlockSpec(memory_space=pltpu.VMEM)
    out_specs = jax.tree.map(lambda _: vmem, out_shape)
    if sent is not None:
        out_specs = tuple(pl.BlockSpec(memory_space=pltpu.HBM) if k == sent else x for k, x in enumerate(out_specs))
    return pl.pallas_call(
        kernel,
        in_specs=[smem] * len(dims) + [vmem] * len(arrays),
        out_specs=out_specs,
        out_shape=out_shape,
        scratch_shapes=scratch,
        name=name,
        compiler_params=pltpu.CompilerParams(vmem_limit_bytes=8 << 20),
    )(*dims, *arrays)


def last_kernel(entries, tot1, tot2, tot3, out_ref):
    r1, r2, r3 = (row_of(t, entries) for t in (tot1, tot2, tot3))
    inv = first_scale(r1)
    values = (
        (inv * inv * one(r1, 0), inv * one(r2, 10), inv * one(r3, 0)),
        (inv * one(r2, 11), one(r2, 0), one(r3, 1)),
        (inv * one(r3, 3), one(r3, 4), one(r3, 2)),
    )
    row = lax.broadcasted_iota(jnp.int32, (3, 3), 0)
    col = lax.broadcasted_iota(jnp.int32, (3, 3), 1)
    out = jnp.zeros((3, 3), f32)
    for i in range(3):
        for j in range(3):
            out = jnp.where((row == i) & (col == j), values[i][j], out)
    out_ref[...] = out


def on_device(psi_start, left_env, right_env, connect, sector_dims, precond):
    blocks, width = psi_start.shape[:2]
    devices = lax.axis_size("sector")
    pieces = lax.axis_size("term")
    share = width // pieces
    entries = float(blocks * devices * width * width)
    everyone = ("term", "sector")
    row = jax.ShapeDtypeStruct((1, 128), f32)
    cut = jax.ShapeDtypeStruct((pieces, blocks, share, width), bf16)
    part = jax.ShapeDtypeStruct((blocks, share, width), f32)
    place = lax.axis_index("sector")
    conn = connect - (place * blocks - blocks)
    turned = (2 - conn // blocks) * blocks + conn % blocks
    conn = jnp.where(place % 2 == 1, turned, conn)

    def exchange(x):
        return lax.all_to_all(x, "term", 0, 0, tiled=True)

    def reduced(stage, partial, *shares):
        mine, sent, sums = call_small(
            lambda *refs: reduce_kernel(stage, *refs),
            [],
            [exchange(partial), *shares],
            (part, pltpu.HBM(part.shape, f32), row),
            f"reduce_{stage}",
            1,
            [pltpu.SemaphoreType.DMA],
        )
        sums = jnp.broadcast_to(sums, (pieces * devices, 128))
        sums, sent = lax.optimization_barrier((sums, sent))
        return (mine, swapped(sent, 1)), lax.all_to_all(sums, everyone, 0, 0, tiled=True)

    def updated(stage, tots, own, far):
        out = (part, part) + ((row,) if stage > 1 else ())
        every = pltpu.HBM((pieces, 2, blocks, share, width), bf16)
        v, v_far, *more, every = call_small(
            lambda *refs: update_kernel(stage, entries, *refs),
            [],
            [*tots, *own, *far],
            (*out, every),
            f"update_{stage}",
            len(out),
            [pltpu.VMEM((2, blocks, share, width), bf16), pltpu.SemaphoreType.DMA((2, pieces))],
        )
        both = exchange(every)
        return (v, v_far), (both, swapped(both[:, 0], 0)), more

    hbm = pl.BlockSpec(memory_space=pltpu.HBM)
    shares = pl.pallas_call(
        share_kernel,
        in_specs=[pl.BlockSpec(memory_space=pltpu.SMEM), hbm, hbm],
        out_specs=hbm,
        out_shape=pltpu.HBM((2, blocks, share, width), bf16),
        scratch_shapes=[pltpu.VMEM((2, blocks, share, width), bf16), pltpu.SemaphoreType.DMA((3,))],
        name="share",
        compiler_params=pltpu.CompilerParams(vmem_limit_bytes=4 << 20),
    )(
        sector_dims,
        pltpu.with_memory_space_constraint(psi_start, pltpu.HBM),
        pltpu.with_memory_space_constraint(precond, pltpu.HBM),
    )
    psi = call_small(start_kernel, [sector_dims], [psi_start], cut, "start")
    far = swapped(shares, 1)
    outside = [pltpu.with_memory_space_constraint(x, pltpu.HBM) for x in (left_env, right_env)]

    groups = (to_everyone(far[0], "term"), psi, swapped(psi, 0))
    partial = product(1, conn, sector_dims, groups, (), *outside)
    sig1, tot1 = reduced(1, partial, shares)
    v2, groups2, _ = updated(1, (tot1,), (shares, sig1[0]), (far, sig1[1]))

    partial = product(2, conn, sector_dims, groups2, (), left_env, right_env)
    sig2, tot2 = reduced(2, partial, shares, sig1[0], v2[0])
    v3, groups3, (more,) = updated(2, (tot1, tot2), (shares, sig1[0], sig2[0], v2[0]), (far, sig1[1], sig2[1], v2[1]))

    row3 = product(3, conn, sector_dims, groups3, (psi, groups2[0], more), left_env, right_env)
    tot3 = to_everyone(row3[0], everyone)
    env = product(4, conn, sector_dims, groups3, (), left_env)
    projected = call_small(
        lambda *refs: last_kernel(entries, *refs), [], [tot1, tot2, tot3], jax.ShapeDtypeStruct((3, 3), f32), "last"
    )
    return (projected, v3[0], env)


def solution(mesh):
    placed = (
        P("sector", None, None),
        P("term", "sector", None, None),
        P("term", "sector", None, None),
        P("term", "sector"),
        P(None, "sector"),
        P("sector", None, None),
    )
    return jax.shard_map(
        on_device,
        mesh=mesh,
        in_specs=placed,
        out_specs=(P(), P("sector", "term", None), P("term", "sector", None, None)),
        check_vma=False,
    )
```

```python
import jax
import jax.numpy as jnp
from jax import lax
from jax.experimental import pallas as pl
from jax.experimental.pallas import tpu as pltpu
from jax.sharding import PartitionSpec as P

epsilon = 1e-06
f32 = jnp.float32
bf16 = jnp.bfloat16


def to_everyone(x, axis):
    devices = lax.axis_size(axis)
    return lax.all_to_all(jnp.broadcast_to(x[None], (devices, *x.shape)), axis, 0, 0, tiled=True)


def swapped(block, first):
    pairs = [(i, i + 1) for i in range(first, lax.axis_size("sector") - 1, 2)]
    return lax.ppermute(block, "sector", pairs + [(j, i) for i, j in pairs])


def row_of(total_ref, entries):
    return jnp.sum(total_ref[...], axis=0, keepdims=True) * (1.0 / entries)


def one(row, k):
    return row[:, k : k + 1]


def first_scale(row1):
    return 1.0 / jnp.sqrt(one(row1, 6) + epsilon)


def second_weights(row1):
    inv = first_scale(row1)
    theta, a, b, aa, ab, bb, vv = (inv * inv * one(row1, k) for k in range(7))
    o = a - theta * b
    length = aa + theta * theta * bb + o * o * vv - 2.0 * theta * ab - 2.0 * o * a + 2.0 * theta * o * b
    r = 1.0 / jnp.sqrt(jnp.maximum(length, 0.0) + epsilon)
    return r * inv, -r * theta * inv, -r * o * inv


def third_weights(row1, row2):
    inv = first_scale(row1)
    theta = one(row2, 0)
    v1a = inv * one(row2, 1)
    v1b = inv * one(row2, 2)
    v2a = one(row2, 3)
    v2b = one(row2, 4)
    aa = one(row2, 5)
    ab = one(row2, 6)
    bb = one(row2, 7)
    v1v2 = inv * one(row2, 8)
    v2v2 = one(row2, 9)
    v1v1 = inv * inv * one(row1, 6)
    o1 = v1a - theta * v1b
    o2 = v2a - theta * v2b
    length = (
        aa
        - 2.0 * theta * ab
        + theta * theta * bb
        - 2.0 * o1 * o1
        - 2.0 * o2 * o2
        + o1 * o1 * v1v1
        + 2.0 * o1 * o2 * v1v2
        + o2 * o2 * v2v2
    )
    r = 1.0 / jnp.sqrt(jnp.maximum(length, 0.0) + epsilon)
    return r, -r * theta, -r * o1 * inv, -r * o2


def fold(x):
    return jnp.sum(x.reshape(x.shape[0] // 8, 8, x.shape[1]), axis=0)


def row_from(sums):
    lane = lax.broadcasted_iota(jnp.int32, (1, 128), 1)
    row = jnp.zeros((1, 128), f32)
    for k, total in enumerate(sums):
        row = row + jnp.where(lane == k, jnp.sum(total), 0.0)
    return row


def keep_of(dims_ref, s, width):
    rows = lax.broadcasted_iota(jnp.int32, (width, width), 0)
    cols = lax.broadcasted_iota(jnp.int32, (width, width), 1)
    return (rows < dims_ref[0, s]) & (cols < dims_ref[1, s])


def masked(x, dims_ref, s, first):
    rows = lax.broadcasted_iota(jnp.int32, x.shape, 0)
    cols = lax.broadcasted_iota(jnp.int32, x.shape, 1)
    keep = (rows < dims_ref[0, s] - first) & (cols < dims_ref[1, s])
    return jnp.where(keep, x.astype(f32), 0.0).astype(bf16)


def share_kernel(dims_ref, psi_ref, d_ref, shares_ref, buf_ref, sem):
    blocks, share = buf_ref.shape[1:3]
    first = lax.axis_index("term") * share
    mine = pl.ds(pl.multiple_of(first, share), share)
    copies = [pltpu.make_async_copy(x.at[:, mine], buf_ref.at[k], sem.at[k]) for k, x in enumerate((psi_ref, d_ref))]
    for copy in copies:
        copy.start()
    for copy in copies:
        copy.wait()
    for s in range(blocks):
        buf_ref[0, s] = masked(buf_ref[0, s], dims_ref, s, first)
    copy = pltpu.make_async_copy(buf_ref, shares_ref, sem.at[2])
    copy.start()
    copy.wait()


def start_kernel(dims_ref, psi_ref, out_ref):
    pieces, blocks, share = out_ref.shape[:3]

    def body(s, carry):
        for p in range(pieces):
            out_ref[p, s] = masked(psi_ref[s, pl.ds(p * share, share)], dims_ref, s, p * share)
        return carry

    lax.fori_loop(0, blocks, body, 0)


def reduce_kernel(stage, arrived_ref, shares_ref, *refs):
    if stage > 1:
        sig1_ref, v2_ref, refs = refs[0], refs[1], refs[2:]
    mine_ref, send_ref, row_ref, sem = refs
    pieces, blocks, share, width = arrived_ref.shape

    def body(s, acc):
        sig = arrived_ref[0, s].astype(f32)
        for p in range(1, pieces):
            sig = sig + arrived_ref[p, s].astype(f32)
        mine_ref[s] = sig
        psi = shares_ref[0, s].astype(f32)
        rd = 1.0 / shares_ref[1, s].astype(f32)
        a = sig * rd
        if stage == 1:
            b = psi * rd
            terms = (psi * sig, psi * a, psi * b, a * a, a * b, b * b, psi * psi)
        else:
            v2 = v2_ref[s]
            b = v2 * rd
            terms = (
                v2 * sig,
                psi * a,
                psi * b,
                v2 * a,
                v2 * b,
                a * a,
                a * b,
                b * b,
                psi * v2,
                v2 * v2,
                psi * sig,
                v2 * sig1_ref[s],
            )
        return tuple(t + fold(x) for t, x in zip(acc, terms))

    acc = lax.fori_loop(0, blocks, body, (jnp.zeros((8, width), f32),) * (7 if stage == 1 else 12))
    copy = pltpu.make_async_copy(mine_ref, send_ref, sem)
    copy.start()
    row_ref[...] = row_from(acc)
    copy.wait()


def update_kernel(stage, entries, *refs):
    tots, refs = refs[:stage], refs[stage:]
    per = 2 if stage == 1 else 4
    groups, refs = (refs[:per], refs[per : 2 * per]), refs[2 * per :]
    v_refs, refs = refs[: 3 - stage], refs[3 - stage :]
    if stage > 1:
        row_ref, refs = refs[0], refs[1:]
    all_ref, buf_ref, sem = refs
    pieces, _, blocks, share, width = all_ref.shape
    rows = [row_of(t, entries) for t in tots]
    if stage == 1:
        p, q, w = (x[0, 0] for x in second_weights(*rows))
    else:
        p, q, w, y = (x[0, 0] for x in third_weights(*rows))
    copies = []
    for g in range(2):

        def body(s, acc, g=g):
            psi = groups[g][0][0, s].astype(f32)
            rd = 1.0 / groups[g][0][1, s].astype(f32)
            sig1 = groups[g][1][s]
            if stage == 1:
                v = (p * sig1 + q * psi) * rd + w * psi
            else:
                sig2, v2 = groups[g][2][s], groups[g][3][s]
                v = (p * sig2 + q * v2) * rd + w * psi + y * v2
                acc = acc[0] + fold(v * sig1), acc[1] + fold(v * sig2)
            if g < len(v_refs):
                v_refs[g][s] = v
            buf_ref[g, s] = v.astype(bf16)
            return acc

        acc = lax.fori_loop(0, blocks, body, (jnp.zeros((8, width), f32),) * (0 if stage == 1 else 2))
        if stage > 1 and g == 0:
            zero = jnp.zeros((8, width), f32)
            row_ref[...] = row_from([zero, zero, zero, *acc])
        for k in range(pieces):
            copies.append(pltpu.make_async_copy(buf_ref.at[g], all_ref.at[k, g], sem.at[g, k]))
            copies[-1].start()
    for copy in copies:
        copy.wait()


def dot(a, b, ca, cb):
    return lax.dot_general(a, b, (((ca,), (cb,)), ((), ())), preferred_element_type=f32)


together = 2


def product_kernel(stage, *refs):
    conn_ref, dims_ref, groups, refs = refs[0], refs[1], refs[2 : 4 + (stage == 1)], refs[4 + (stage == 1) :]
    if stage == 1:
        far_ref, own_ref, near_ref = groups
    else:
        own_ref, far_ref, near_ref = groups[0].at[:, 0], groups[0].at[:, 1], groups[1]
    if stage == 3:
        psi_ref, v2_ref, part_ref, refs = refs[0], refs[1], refs[2], refs[3:]
    sources = refs[: 1 if stage == 4 else 2]
    refs = refs[len(sources) :]
    out_ref, vb_ref = refs[:2]
    sides = sources
    incoming = []
    if stage == 1:
        sides, in_sem = refs[2:4], refs[4]
        for g in range(sources[0].shape[1] // together):
            at = pl.ds(g * together, together)
            incoming += [
                pltpu.make_async_copy(x.at[:, at], y.at[:, at], in_sem.at[k, g]) for k, (x, y) in enumerate(zip(sources, sides))
            ]
    for copy in incoming:
        copy.start()
    if stage != 3:
        buf_ref, out_sem = refs[-2:]
    pieces, blocks, share, width = own_ref.shape
    terms = sources[0].shape[0]
    steps = blocks // together
    def body(s, carry):
        for seg, ref in enumerate((far_ref, own_ref, near_ref)):
            vb_ref[seg * blocks + s] = ref[:, s].reshape(width, width)
        return carry

    lax.fori_loop(0, blocks, body, 0)
    outgoing = []
    sums = [jnp.zeros((8, width), f32)] * 3
    for g in range(steps):
        here = range(g * together, (g + 1) * together)
        for copy in incoming[2 * g : 2 * g + 2]:
            copy.wait()
        halves = {
            s: [dot(sides[0][t, s], vb_ref[conn_ref[t, s]], 1, 0).astype(bf16) for t in range(terms)] for s in here
        }
        for s in here:
            if stage == 4:
                own_t = vb_ref[blocks + s].T
                for t in range(terms):
                    buf_ref[t, s] = (dot(own_t, halves[s][t], 1, 0) * width ** (-0.5)).astype(bf16)
                continue
            side = jnp.concatenate([sides[1][t, s] for t in range(terms)], axis=1)
            total = dot(jnp.concatenate(halves[s], axis=1), side, 1, 1)
            if stage < 3:
                total = jnp.where(keep_of(dims_ref, s, width), total, 0.0).astype(bf16)
                buf_ref[:, s] = total.reshape(pieces, share, width)
            else:
                for p in range(pieces):
                    part = total[p * share : (p + 1) * share]
                    for k, x in enumerate((psi_ref[p, s], v2_ref[p, 0, s], own_ref[p, s])):
                        sums[k] = sums[k] + fold(x.astype(f32) * part)
        if stage != 3:
            at = pl.ds(g * together, together)
            outgoing.append(pltpu.make_async_copy(buf_ref.at[:, at], out_ref.at[:, at], out_sem.at[g]))
            outgoing[-1].start()
    for copy in outgoing:
        copy.wait()
    if stage == 3:
        out_ref[...] = row_from(sums) + part_ref[...]


def product(stage, conn, dims, groups, more, *sides):
    terms, blocks, width = sides[0].shape[:3]
    pieces, share = groups[-1].shape[0], groups[-1].shape[2]
    smem = pl.BlockSpec(memory_space=pltpu.SMEM)
    vmem = pl.BlockSpec(memory_space=pltpu.VMEM)
    hbm = pl.BlockSpec(memory_space=pltpu.HBM)
    steps = blocks // together
    scratch = [pltpu.VMEM((3 * blocks, width, width), bf16)]
    if stage == 1:
        scratch += [pltpu.VMEM(x.shape, bf16) for x in sides]
        scratch.append(pltpu.SemaphoreType.DMA((2, steps)))
    if stage == 3:
        out_shape, out_specs = jax.ShapeDtypeStruct((1, 128), f32), vmem
    else:
        shape = sides[0].shape if stage == 4 else (pieces, blocks, share, width)
        out_shape, out_specs = pltpu.HBM(shape, bf16), hbm
        scratch += [pltpu.VMEM(shape, bf16), pltpu.SemaphoreType.DMA((steps,))]
    return pl.pallas_call(
        lambda *refs: product_kernel(stage, *refs),
        in_specs=[smem, smem] + [vmem] * (len(groups) + len(more)) + [hbm if stage == 1 else vmem] * len(sides),
        out_specs=out_specs,
        out_shape=out_shape,
        scratch_shapes=scratch,
        name=f"product_{stage}",
        compiler_params=pltpu.CompilerParams(vmem_limit_bytes=12 << 20),
    )(conn, dims, *groups, *more, *sides)


def keep_kernel(here_ref, there_ref, sem):
    copies = [pltpu.make_async_copy(here_ref.at[t], there_ref.at[t], sem.at[t]) for t in range(here_ref.shape[0])]
    for copy in copies:
        copy.start()
    for copy in copies:
        copy.wait()


def kept(x):
    return pl.pallas_call(
        keep_kernel,
        in_specs=[pl.BlockSpec(memory_space=pltpu.HBM)],
        out_specs=pl.BlockSpec(memory_space=pltpu.VMEM),
        out_shape=pltpu.VMEM(x.shape, x.dtype),
        scratch_shapes=[pltpu.SemaphoreType.DMA((x.shape[0],))],
        name="keep",
        compiler_params=pltpu.CompilerParams(vmem_limit_bytes=1 << 20),
    )(pltpu.with_memory_space_constraint(x, pltpu.HBM))


def call_small(kernel, dims, arrays, out_shape, name, sent=None, scratch=()):
    smem = pl.BlockSpec(memory_space=pltpu.SMEM)
    vmem = pl.BlockSpec(memory_space=pltpu.VMEM)
    out_specs = jax.tree.map(lambda _: vmem, out_shape)
    if sent is not None:
        out_specs = tuple(pl.BlockSpec(memory_space=pltpu.HBM) if k == sent else x for k, x in enumerate(out_specs))
    return pl.pallas_call(
        kernel,
        in_specs=[smem] * len(dims) + [vmem] * len(arrays),
        out_specs=out_specs,
        out_shape=out_shape,
        scratch_shapes=scratch,
        name=name,
        compiler_params=pltpu.CompilerParams(vmem_limit_bytes=8 << 20),
    )(*dims, *arrays)


def last_kernel(entries, tot1, tot2, tot3, out_ref):
    r1, r2, r3 = (row_of(t, entries) for t in (tot1, tot2, tot3))
    inv = first_scale(r1)
    values = (
        (inv * inv * one(r1, 0), inv * one(r2, 10), inv * one(r3, 0)),
        (inv * one(r2, 11), one(r2, 0), one(r3, 1)),
        (inv * one(r3, 3), one(r3, 4), one(r3, 2)),
    )
    row = lax.broadcasted_iota(jnp.int32, (3, 3), 0)
    col = lax.broadcasted_iota(jnp.int32, (3, 3), 1)
    out = jnp.zeros((3, 3), f32)
    for i in range(3):
        for j in range(3):
            out = jnp.where((row == i) & (col == j), values[i][j], out)
    out_ref[...] = out


def on_device(psi_start, left_env, right_env, connect, sector_dims, precond):
    blocks, width = psi_start.shape[:2]
    devices = lax.axis_size("sector")
    pieces = lax.axis_size("term")
    share = width // pieces
    entries = float(blocks * devices * width * width)
    everyone = ("term", "sector")
    row = jax.ShapeDtypeStruct((1, 128), f32)
    cut = jax.ShapeDtypeStruct((pieces, blocks, share, width), bf16)
    part = jax.ShapeDtypeStruct((blocks, share, width), f32)
    place = lax.axis_index("sector")
    conn = connect - (place * blocks - blocks)
    turned = (2 - conn // blocks) * blocks + conn % blocks
    conn = jnp.where(place % 2 == 1, turned, conn)

    def exchange(x):
        return lax.all_to_all(x, "term", 0, 0, tiled=True)

    def reduced(stage, partial, *shares):
        mine, sent, sums = call_small(
            lambda *refs: reduce_kernel(stage, *refs),
            [],
            [exchange(partial), *shares],
            (part, pltpu.HBM(part.shape, f32), row),
            f"reduce_{stage}",
            1,
            [pltpu.SemaphoreType.DMA],
        )
        sums = jnp.broadcast_to(sums, (pieces * devices, 128))
        sums, sent = lax.optimization_barrier((sums, sent))
        return (mine, swapped(sent, 1)), lax.all_to_all(sums, everyone, 0, 0, tiled=True)

    def updated(stage, tots, own, far):
        out = (part, part) if stage == 1 else (part, row)
        every = pltpu.HBM((pieces, 2, blocks, share, width), bf16)
        v, other, every = call_small(
            lambda *refs: update_kernel(stage, entries, *refs),
            [],
            [*tots, *own, *far],
            (*out, every),
            f"update_{stage}",
            len(out),
            [pltpu.VMEM((2, blocks, share, width), bf16), pltpu.SemaphoreType.DMA((2, pieces))],
        )
        both = exchange(every)
        return v, other, (both, swapped(both[:, 0], 0))

    hbm = pl.BlockSpec(memory_space=pltpu.HBM)
    shares = pl.pallas_call(
        share_kernel,
        in_specs=[pl.BlockSpec(memory_space=pltpu.SMEM), hbm, hbm],
        out_specs=hbm,
        out_shape=pltpu.HBM((2, blocks, share, width), bf16),
        scratch_shapes=[pltpu.VMEM((2, blocks, share, width), bf16), pltpu.SemaphoreType.DMA((3,))],
        name="share",
        compiler_params=pltpu.CompilerParams(vmem_limit_bytes=4 << 20),
    )(
        sector_dims,
        pltpu.with_memory_space_constraint(psi_start, pltpu.HBM),
        pltpu.with_memory_space_constraint(precond, pltpu.HBM),
    )
    psi = call_small(start_kernel, [sector_dims], [psi_start], cut, "start")
    far = swapped(shares, 1)
    outside = [pltpu.with_memory_space_constraint(x, pltpu.HBM) for x in (left_env, right_env)]

    groups = (to_everyone(far[0], "term"), psi, swapped(psi, 0))
    partial = product(1, conn, sector_dims, groups, (), *outside)
    sig1, tot1 = reduced(1, partial, shares)
    v2, v2_far, groups2 = updated(1, (tot1,), (shares, sig1[0]), (far, sig1[1]))

    partial = product(2, conn, sector_dims, groups2, (), left_env, right_env)
    sig2, tot2 = reduced(2, partial, shares, sig1[0], v2)
    v3, more, groups3 = updated(2, (tot1, tot2), (shares, sig1[0], sig2[0], v2), (far, sig1[1], sig2[1], v2_far))

    row3 = product(3, conn, sector_dims, groups3, (psi, groups2[0], more), left_env, right_env)
    tot3 = to_everyone(row3[0], everyone)
    env = product(4, conn, sector_dims, groups3, (), left_env)
    projected = call_small(
        lambda *refs: last_kernel(entries, *refs), [], [tot1, tot2, tot3], jax.ShapeDtypeStruct((3, 3), f32), "last"
    )
    return (projected, v3, env)


def solution(mesh):
    placed = (
        P("sector", None, None),
        P("term", "sector", None, None),
        P("term", "sector", None, None),
        P("term", "sector"),
        P(None, "sector"),
        P("sector", None, None),
    )
    return jax.shard_map(
        on_device,
        mesh=mesh,
        in_specs=placed,
        out_specs=(P(), P("sector", "term", None), P("term", "sector", None, None)),
        check_vma=False,
    )
```
